32 devices in a mesh: dp: 2 (over y), seq: 16 (over z, x, core).
Axes of the slice: x: 2, y: 2, z: 4, core: 2. Of those that a mesh axis runs over, the one named last changes fastest.
Arguments:
- layer_input: bfloat16 [2, 2048, 1024], P('dp', 'seq'), may hold values from -12 to 12
- v_first: bfloat16 [2, 2048, 1024], P('dp', 'seq'), may hold values from -6 to 6
- cotangent: bfloat16 [2, 2048, 1024], P('dp', 'seq'), may hold values from -6 to 6
- segments: int32 [2, 2048], P('dp'), may hold values from 0 to 3, never falling along the last dimension, each value on 1 to 1024 neighbouring positions
- norm1_gain: bfloat16 [1024], P('seq'), may hold values from 0.099609375 to 1.8984375
- w_query: bfloat16 [1024, 1024], P('seq', 'dp'), may hold values from -0.1875 to 0.1875
- w_key: bfloat16 [1024, 1024], P('seq', 'dp'), may hold values from -0.1875 to 0.1875
- w_value: bfloat16 [1024, 1024], P('seq', 'dp'), may hold values from -0.1875 to 0.1875
- w_out: bfloat16 [1024, 1024], P('seq', 'dp'), may hold values from -1.5 to 1.5
- norm2_gain: bfloat16 [1024], P('seq'), may hold values from 0.099609375 to 1.8984375
- w_gate: bfloat16 [1024, 2816], P('seq', 'dp'), may hold values from -0.1875 to 0.1875
- w_up: bfloat16 [1024, 2816], P('seq', 'dp'), may hold values from -0.1875 to 0.1875
- w_down: bfloat16 [2816, 1024], P('seq', 'dp'), may hold values from -0.109375 to 0.109375
Outputs:
- out: bfloat16 [2, 2048, 1024], P('dp', 'seq')
- d_input: bfloat16 [2, 2048, 1024], P('dp', 'seq')
- d_v_first: bfloat16 [2, 2048, 1024], P('dp', 'seq')
- d_norm1_gain: float32 [1024], P('seq')
- d_w_query: float32 [1024, 1024], P('seq', 'dp')
- d_w_key: float32 [1024, 1024], P('seq', 'dp')
- d_w_value: float32 [1024, 1024], P('seq', 'dp')
- d_w_out: float32 [1024, 1024], P('seq', 'dp')
- d_norm2_gain: float32 [1024], P('seq')
- d_w_gate: float32 [1024, 2816], P('seq', 'dp')
- d_w_up: float32 [1024, 2816], P('seq', 'dp')
- d_w_down: float32 [2816, 1024], P('seq', 'dp')
- rms: float32 [3], replicated
The draws below stay inside these ranges and needn't reach their ends.
Inputs may be any that keep to these rules, and one draw needn't show every extreme that they name: `segments`: in each row the ids start at 0 and never fall; every id up to 3 is used, by at most 1024 tokens.
All inputs are finite; a program needn't handle non-finite values.
Results may differ from the reference program's by a relative error of at most 0.022.
Values may be sent and summed in bfloat16 or wider, within the bound.
No kernel may reach another device: no remote copies, remote signals or barrier semaphores. Data moves between devices by JAX's collectives and lax.ppermute only.
A program may use at most 256 MiB of HBM per device.

```python
import math
import jax
import jax.numpy as jnp
import numpy as np
from jax import lax

D = 1024
H = 16
HS = 64
FF = 2816
DOCS = 4
HD = 1024
LENGTH = 2048
SEQ_TOTAL = 2


def draw_layer_input(key, part):
    shape = (SEQ_TOTAL, LENGTH, D)
    along_rows = jnp.arange(LENGTH, dtype=jnp.float32) / LENGTH
    across_seqs = jnp.arange(SEQ_TOTAL, dtype=jnp.float32) / SEQ_TOTAL
    spread_rows = jnp.exp(math.log(3.0) * (along_rows[None, :] + across_seqs[:, None] - 1.0))
    base_draw = jax.random.truncated_normal(key, -4.0, 4.0, shape, jnp.float32)
    return (base_draw * spread_rows[:, :, None]).astype(jnp.bfloat16)


def block_levels(rng, shape, cuts, low, top_value):
    def one(axis_at, blocks):
        draws = jax.random.uniform(jax.random.fold_in(jax.random.fold_in(rng, 6), axis_at), (blocks,), jnp.float32, low / len(cuts), top_value / len(cuts))
        return jnp.repeat(jnp.exp(draws), shape[axis_at] // blocks).reshape((-1,) + (1,) * (len(shape) - axis_at - 1))

    gain = one(*cuts[0])
    for cut in cuts[1:]:
        gain = gain * one(*cut)
    return gain


def split_up(number_of, total, limit, lean):
    loads = [(1 << 20) // math.isqrt(grade ** lean) + 1 for grade in range(2, number_of + 1)]
    spare, holding = total - limit - (number_of - 1), [1] * (number_of - 1)
    while spare > 0:
        free = [i for i in range(number_of - 1) if holding[i] < limit]
        mass, remaining = sum([loads[i] for i in free]), spare
        for i in free:
            extra = min(limit - holding[i], max(1, remaining * loads[i] // mass), spare)
            holding[i] = holding[i] + extra
            spare = spare - extra
    return np.array([limit] + holding)


def uneven_parts(stream_key, number_of, total, reach, slope):
    if number_of == 2:
        one = jax.random.randint(stream_key, (), max(1, total - reach), min(reach, total - 1) + 1)
        return jnp.stack([one, total - one])
    lengths = jnp.asarray(split_up(number_of, total, reach, slope), jnp.int32)
    twos = (number_of - 1) // 2
    source_of, sink = lengths[1:1 + 2 * twos:2], lengths[2:2 + 2 * twos:2]
    slack = jnp.minimum(source_of - 1, reach - sink)
    passed = jax.random.randint(jax.random.fold_in(stream_key, 1), (twos,), 0, 1 << 20) % (slack + 1)
    lengths = lengths.at[1:1 + 2 * twos:2].set(source_of - passed).at[2:2 + 2 * twos:2].set(sink + passed)
    return lengths[jax.random.permutation(jax.random.fold_in(stream_key, 2), number_of)]


def scatter_about(key, shape, width, reach, cuts=(), kind=jnp.bfloat16):
    entries = width * jax.random.normal(key, shape, jnp.float32)
    if cuts:
        entries = entries * block_levels(key, shape, cuts, -0.22, 0.18)
    return jnp.clip(entries, -reach, reach).astype(kind)


def setup_inputs(seed: int = 0) -> dict:
    key_of = jax.random.split(jax.random.key(seed), 14)
    return {
        "layer_input": draw_layer_input(jax.random.fold_in(key_of[13], 71), 0),
        "v_first": scatter_about(key_of[1], (SEQ_TOTAL, LENGTH, HD), 1.0, 6.0, ((0, 2), (1, 16))),
        "cotangent": scatter_about(key_of[2], (SEQ_TOTAL, LENGTH, D), 1.0, 6.0, ((0, 2), (1, 16))),
        "segments": jax.vmap(lambda own: jnp.searchsorted(jnp.cumsum(uneven_parts(own, DOCS, LENGTH, LENGTH // 2, 1)), jnp.arange(LENGTH), side="right"))(jax.random.split(key_of[3], SEQ_TOTAL)).reshape((SEQ_TOTAL, LENGTH)).astype(jnp.int32),
        "norm1_gain": jnp.clip(1.0 + 0.18 * jax.random.normal(key_of[4], (D,), jnp.float32), 0.099609375, 1.8984375).astype(jnp.bfloat16),
        "w_query": scatter_about(key_of[5], (D, HD), D ** -0.5, 0.1875, ((0, 16), (1, 2))),
        "w_key": scatter_about(key_of[6], (D, HD), D ** -0.5, 0.1875, ((0, 16), (1, 2))),
        "w_value": scatter_about(key_of[7], (D, HD), D ** -0.5, 0.1875, ((0, 16), (1, 2))),
        "w_out": scatter_about(key_of[8], (HD, D), (HD // 64) ** -0.5, 1.5, ((0, 16), (1, 2))),
        "norm2_gain": jnp.clip(1.0 + 0.18 * jax.random.normal(key_of[9], (D,), jnp.float32), 0.099609375, 1.8984375).astype(jnp.bfloat16),
        "w_gate": scatter_about(key_of[10], (D, FF), D ** -0.5, 0.1875, ((0, 16), (1, 2))),
        "w_up": scatter_about(key_of[11], (D, FF), D ** -0.5, 0.1875, ((0, 16), (1, 2))),
        "w_down": scatter_about(key_of[12], (FF, D), FF ** -0.5, 0.109375, ((0, 16), (1, 2))),
    }


EPSILON = 1e-06

@jax.custom_vjp
def low(v):
    return lax.optimization_barrier(v.astype(jnp.bfloat16)).astype(jnp.float32)

@jax.custom_vjp
def low_back(v):
    return v

def low_keep(v):
    return (low(v), None)

def low_pass(kept, grad):
    return (grad,)

def back_keep(v):
    return (v, None)

def back_low(kept, grad):
    return (low(grad),)
low.defvjp(low_keep, low_pass)
low_back.defvjp(back_keep, back_low)

def product(left_rows, right_rows):
    return jnp.dot(left_rows, right_rows, precision=lax.Precision.HIGHEST)

def normalize(rows_in, gain_in):
    return rows_in * lax.rsqrt(lax.optimization_barrier(jnp.mean(rows_in * rows_in, axis=-1, keepdims=True)) + EPSILON) * gain_in

def rotary(values, positions):
    half_size = HS // 2
    frequency = 10000.0 ** (-jnp.arange(half_size, dtype=jnp.float32) * 2.0 / HS)
    angles = positions[:, None] * frequency[None, :]
    cosine = jnp.cos(angles)[:, None, :]
    sine_t = jnp.sin(angles)[:, None, :]
    shaped = values.reshape(values.shape[0], H, HS)
    lower_half = shaped[..., :half_size]
    upper_half = shaped[..., half_size:]
    turned = jnp.concatenate([lower_half * cosine - upper_half * sine_t, upper_half * cosine + lower_half * sine_t], axis=-1)
    return turned.reshape(values.shape)

def attend(q_rot, k_rot, mixed_values, segment_row):
    length = q_rot.shape[0]
    block_rows = min(512, length)
    score_scale = HS ** (-0.5)
    keys_h = k_rot.reshape(length, H, HS)
    values_h = mixed_values.reshape(length, H, HS)
    key_index = jnp.arange(length, dtype=jnp.int32)
    blocks_query = q_rot.reshape(length // block_rows, block_rows, H, HS)
    blocks_segment = segment_row.reshape(length // block_rows, block_rows)
    blocks_index = key_index.reshape(length // block_rows, block_rows)

    def one_block(item_in):
        query_block, segment_block, index_block = item_in
        raw_scores = jnp.einsum('qhd,khd->hqk', query_block, keys_h, precision=lax.Precision.HIGHEST) * score_scale
        raw_scores = low_back(raw_scores)
        allowed = (segment_block[:, None] == segment_row[None, :]) & (key_index[None, :] <= index_block[:, None])
        masked = jnp.where(allowed[None], raw_scores, -1e+30)
        soft_weights = low(jax.nn.softmax(masked, axis=-1))
        return jnp.einsum('hqk,khd->qhd', soft_weights, values_h, precision=lax.Precision.HIGHEST)
    attended = lax.map(jax.checkpoint(one_block), (blocks_query, blocks_segment, blocks_index))
    return attended.reshape(length, H * HS)

def decoder_layer(rows_in, first_values, segment_row, weights):
    gain_one, w_query, w_key, w_value, w_out, gain_two, w_gate, w_up, w_down = weights
    length = rows_in.shape[0]
    token_index = jnp.arange(length, dtype=jnp.int32)
    starts = lax.optimization_barrier(jnp.sum((segment_row[None, :] < segment_row[:, None]).astype(jnp.int32), axis=1))
    positions = (token_index - starts).astype(jnp.float32)
    normed_one = low(normalize(rows_in, gain_one))
    query_raw = low_back(product(normed_one, w_query))
    key_raw = low_back(product(normed_one, w_key))
    mixed_values = low_back(0.5 * product(normed_one, w_value) + 0.5 * first_values)
    q_rot = low(rotary(query_raw, positions))
    k_rot = low(rotary(key_raw, positions))
    attended = low(low_back(attend(q_rot, k_rot, low(mixed_values), segment_row)))
    branch_a = low_back(product(attended, w_out))
    hidden_in = rows_in + branch_a
    normed_two = low(normalize(hidden_in, gain_two))
    gate_pre = low_back(product(normed_two, w_gate))
    upward = low_back(product(normed_two, w_up))
    activated = low(jax.nn.silu(gate_pre) * upward)
    branch_m = product(activated, w_down)
    result = hidden_in + branch_m
    squares = jnp.stack([jnp.sum(result * result), jnp.sum(branch_a * branch_a), jnp.sum(branch_m * branch_m)])
    return (result, squares)

def reference(layer_input, v_first, cotangent, segments, norm1_gain, w_query, w_key, w_value, w_out, norm2_gain, w_gate, w_up, w_down):
    weights = tuple((single.astype(jnp.float32) for single in (norm1_gain, w_query, w_key, w_value, w_out, norm2_gain, w_gate, w_up, w_down)))
    rows_all = layer_input.astype(jnp.float32)
    values_all = v_first.astype(jnp.float32)

    def forward(rows_all, values_all, weights):

        def step_one(carried, item_in):
            rows_in, first_values, segment_row = item_in
            result, squares = decoder_layer(rows_in, first_values, segment_row, weights)
            return (carried + squares, result)
        squares, results = lax.scan(jax.checkpoint(step_one), jnp.zeros((3,), jnp.float32), (rows_all, values_all, segments))
        return (results, squares)
    results, pullback, squares = jax.vjp(forward, rows_all, values_all, weights, has_aux=True)
    d_rows, d_values, d_weights = pullback(cotangent.astype(jnp.float32))
    cell_count = results.shape[0] * results.shape[1] * results.shape[2]
    root_mean = jnp.sqrt(squares / cell_count)
    return (results.astype(jnp.bfloat16), d_rows.astype(jnp.bfloat16), d_values.astype(jnp.bfloat16), d_weights[0], d_weights[1], d_weights[2], d_weights[3], d_weights[4], d_weights[5], d_weights[6], d_weights[7], d_weights[8], root_mean)
```

```python
import jax
import jax.numpy as jnp
from jax import lax
from jax.experimental import pallas as pl
from jax.experimental.pallas import tpu as pltpu
from jax.sharding import Mesh
from jax.sharding import PartitionSpec as P


H = 16
HS = 64


EPSILON = 1e-06


def normalize(rows_in, gain_in):
    return (
        rows_in * lax.rsqrt(jnp.mean(rows_in * rows_in, axis=-1, keepdims=True) + EPSILON) * gain_in
    )


def rotary_tables(positions):
    half_size = HS // 2
    frequency = 10000.0 ** (-jnp.arange(half_size, dtype=jnp.float32) * 2.0 / HS)
    angles = positions[..., None] * frequency
    return (jnp.cos(angles)[..., None, :], jnp.sin(angles)[..., None, :])


def rotate(values, cosine, sine_t):
    shaped = values.reshape(values.shape[:-1] + (H, HS))
    half_size = HS // 2
    lower_half = shaped[..., :half_size]
    upper_half = shaped[..., half_size:]
    turned = jnp.concatenate(
        [lower_half * cosine - upper_half * sine_t, upper_half * cosine + lower_half * sine_t],
        axis=-1,
    )
    return turned.reshape(values.shape)


def project(rows_in, weight):
    return jnp.einsum("sqi,ij->sqj", rows_in, weight, preferred_element_type=jnp.float32)


def project_back(grad_rows, weight):
    return jnp.einsum("sqj,ij->sqi", grad_rows, weight, preferred_element_type=jnp.float32)


def weight_grad(left_rows, right_rows):
    return jnp.einsum("sqi,sqj->ij", left_rows, right_rows, preferred_element_type=jnp.float32)


def fetch_forward(w_query, w_key, w_value, w_out, w_gate, w_up, w_down, norm1_gain, norm2_gain):
    wide_set = (
        lax.all_gather(w_query, "dp", axis=1, tiled=True),
        lax.all_gather(w_key, "dp", axis=1, tiled=True),
        lax.all_gather(w_value, "dp", axis=1, tiled=True),
        lax.all_gather(w_out, "dp", axis=1, tiled=True),
        lax.all_gather(w_gate, "dp", axis=1, tiled=True),
        lax.all_gather(w_up, "dp", axis=1, tiled=True),
        lax.all_gather(w_down, "dp", axis=1, tiled=True),
    )
    return (
        lax.all_gather(wide_set[0], "seq", axis=0, tiled=True),
        lax.all_gather(wide_set[1], "seq", axis=0, tiled=True),
        lax.all_gather(wide_set[2], "seq", axis=0, tiled=True),
        lax.all_gather(wide_set[3], "seq", axis=0, tiled=True),
        lax.all_gather(wide_set[4], "seq", axis=0, tiled=True),
        lax.all_gather(wide_set[5], "seq", axis=0, tiled=True),
        lax.all_gather(wide_set[6], "seq", axis=0, tiled=True),
        lax.all_gather(norm1_gain, "seq", axis=0, tiled=True),
        lax.all_gather(norm2_gain, "seq", axis=0, tiled=True),
    )


def fetch_backward(w_query, w_key, w_value, w_out, w_gate, w_up, w_down, norm1_gain, norm2_gain):
    wide_set = (
        lax.all_gather(w_query, "dp", axis=1, tiled=True),
        lax.all_gather(w_key, "dp", axis=1, tiled=True),
        lax.all_gather(w_value, "dp", axis=1, tiled=True),
        lax.all_gather(w_out, "dp", axis=1, tiled=True),
        lax.all_gather(w_gate, "dp", axis=1, tiled=True),
        lax.all_gather(w_up, "dp", axis=1, tiled=True),
        lax.all_gather(w_down, "dp", axis=1, tiled=True),
    )
    return (
        lax.all_gather(wide_set[0], "seq", axis=0, tiled=True),
        lax.all_gather(wide_set[1], "seq", axis=0, tiled=True),
        lax.all_gather(wide_set[2], "seq", axis=0, tiled=True),
        lax.all_gather(wide_set[3], "seq", axis=0, tiled=True),
        lax.all_gather(wide_set[4], "seq", axis=0, tiled=True),
        lax.all_gather(wide_set[5], "seq", axis=0, tiled=True),
        lax.all_gather(wide_set[6], "seq", axis=0, tiled=True),
        lax.all_gather(norm1_gain, "seq", axis=0, tiled=True),
        lax.all_gather(norm2_gain, "seq", axis=0, tiled=True),
    )


def local(
    layer_input,
    v_first,
    cotangent,
    segments,
    norm1_gain,
    w_query,
    w_key,
    w_value,
    w_out,
    norm2_gain,
    w_gate,
    w_up,
    w_down,
):
    num_seqs, own_tokens, model_width = layer_input.shape
    length = segments.shape[1]
    block_rows = min(1024, length)
    block_count = length // block_rows
    score_scale = HS ** (-0.5)
    offset = lax.axis_index("seq") * own_tokens
    own_seg = lax.dynamic_slice_in_dim(segments, offset, own_tokens, 1)
    own_index = offset + jnp.arange(own_tokens, dtype=jnp.int32)
    starts = jnp.sum((segments[:, None, :] < own_seg[:, :, None]).astype(jnp.int32), axis=2)
    cosine, sine_t = rotary_tables((own_index[None, :] - starts).astype(jnp.float32))
    block_ids = jnp.arange(block_count)
    full_set = fetch_forward(
        w_query, w_key, w_value, w_out, w_gate, w_up, w_down, norm1_gain, norm2_gain
    )
    input_f = layer_input.astype(jnp.float32)
    gain_one = full_set[7].astype(jnp.float32)
    gain_two = full_set[8].astype(jnp.float32)
    normed_one = normalize(input_f, gain_one).astype(jnp.bfloat16)
    query_raw = project(normed_one, full_set[0])
    key_raw = project(normed_one, full_set[1])
    mixed_values = (
        0.5 * project(normed_one, full_set[2]) + 0.5 * v_first.astype(jnp.float32)
    ).astype(jnp.bfloat16)
    q_rot = rotate(query_raw, cosine, sine_t).astype(jnp.bfloat16)
    k_rot = rotate(key_raw, cosine, sine_t).astype(jnp.bfloat16)
    keys_all, values_all = (
        lax.all_gather(k_rot, "seq", axis=1, tiled=True),
        lax.all_gather(mixed_values, "seq", axis=1, tiled=True),
    )
    keys_h = keys_all.reshape(num_seqs, length, H, HS)
    values_h = values_all.reshape(num_seqs, length, H, HS)
    query_h = q_rot.reshape(num_seqs, own_tokens, H, HS)

    def masked_scores(block_no):
        first_row = block_no * block_rows
        key_block = lax.dynamic_slice_in_dim(keys_h, first_row, block_rows, 1)
        value_block = lax.dynamic_slice_in_dim(values_h, first_row, block_rows, 1)
        seg_block = lax.dynamic_slice_in_dim(segments, first_row, block_rows, 1)
        key_index = first_row + jnp.arange(block_rows, dtype=jnp.int32)
        raw_scores = (
            jnp.einsum("sqhd,skhd->shqk", query_h, key_block, preferred_element_type=jnp.float32)
            * score_scale
        )
        allowed = (seg_block[:, None, :] == own_seg[:, :, None]) & (
            key_index[None, None, :] <= own_index[None, :, None]
        )
        return (jnp.where(allowed[:, None], raw_scores, -1e30), key_block, value_block)

    def lse_step(carried, block_no):
        running_max, running_sum = carried
        scores, _, _ = masked_scores(block_no)
        new_max = jnp.maximum(running_max, jnp.max(scores, axis=-1))
        running_sum = running_sum * jnp.exp(running_max - new_max) + jnp.sum(
            jnp.exp(scores - new_max[..., None]), axis=-1
        )
        return ((new_max, running_sum), None)

    stat_shape = (num_seqs, H, own_tokens)
    (running_max, running_sum), _ = lax.scan(
        lse_step,
        (jnp.full(stat_shape, -1e30, jnp.float32), jnp.zeros(stat_shape, jnp.float32)),
        block_ids,
    )
    log_total = running_max + jnp.log(running_sum)

    def attend_step(carried, block_no):
        scores, _, value_block = masked_scores(block_no)
        soft_b = jnp.exp(scores - log_total[..., None]).astype(jnp.bfloat16)
        return (
            carried
            + jnp.einsum(
                "shqk,skhd->sqhd", soft_b, value_block, preferred_element_type=jnp.float32
            ),
            None,
        )

    head_zeros = jnp.zeros((num_seqs, own_tokens, H, HS), jnp.float32)
    attended_f, _ = lax.scan(attend_step, head_zeros, block_ids)
    attended = attended_f.reshape(num_seqs, own_tokens, H * HS).astype(jnp.bfloat16)
    branch_a = project(attended, full_set[3])
    hidden_in = input_f + branch_a
    normed_two = normalize(hidden_in, gain_two).astype(jnp.bfloat16)
    gate_pre = project(normed_two, full_set[4])
    upward = project(normed_two, full_set[5])
    activated = (jax.nn.silu(gate_pre) * upward).astype(jnp.bfloat16)
    branch_m = project(activated, full_set[6])
    result = hidden_in + branch_m
    squares = jnp.stack(
        [jnp.sum(result * result), jnp.sum(branch_a * branch_a), jnp.sum(branch_m * branch_m)]
    )
    reused = fetch_backward(
        w_query, w_key, w_value, w_out, w_gate, w_up, w_down, norm1_gain, norm2_gain
    )
    grad_down = weight_grad(activated, cotangent)
    d_activated = project_back(cotangent, reused[6])
    gate_pull = jax.vjp(lambda gate_in, up_in: jax.nn.silu(gate_in) * up_in, gate_pre, upward)[1]
    d_gate_f, d_upward_f = gate_pull(d_activated)
    d_gate = d_gate_f.astype(jnp.bfloat16)
    d_upward = d_upward_f.astype(jnp.bfloat16)
    grad_gate = weight_grad(normed_two, d_gate)
    grad_up = weight_grad(normed_two, d_upward)
    d_normed_two = project_back(d_gate, reused[4]) + project_back(d_upward, reused[5])
    norm_pull_two = jax.vjp(normalize, hidden_in, gain_two)[1]
    d_hidden_part, d_gain_two = norm_pull_two(d_normed_two)
    d_hidden = cotangent.astype(jnp.float32) + d_hidden_part
    d_branch_a = d_hidden.astype(jnp.bfloat16)
    grad_out = weight_grad(attended, d_branch_a)
    d_attended = project_back(d_branch_a, reused[3]).astype(jnp.bfloat16)
    grad_h = d_attended.reshape(num_seqs, own_tokens, H, HS)

    def delta_step(carried, block_no):
        scores, _, value_block = masked_scores(block_no)
        soft_weights = jnp.exp(scores - log_total[..., None])
        d_soft = jnp.einsum(
            "sqhd,skhd->shqk", grad_h, value_block, preferred_element_type=jnp.float32
        )
        return (carried + jnp.sum(soft_weights * d_soft, axis=-1), None)

    row_delta, _ = lax.scan(delta_step, jnp.zeros(stat_shape, jnp.float32), block_ids)

    def score_grads(block_no):
        scores, key_block, value_block = masked_scores(block_no)
        soft_weights = jnp.exp(scores - log_total[..., None])
        d_soft = jnp.einsum(
            "sqhd,skhd->shqk", grad_h, value_block, preferred_element_type=jnp.float32
        )
        d_scores = (soft_weights * (d_soft - row_delta[..., None])).astype(jnp.bfloat16)
        return (soft_weights.astype(jnp.bfloat16), d_scores, key_block)

    def query_and_key(carried, block_no):
        soft_b, d_scores, key_block = score_grads(block_no)
        carried = carried + jnp.einsum(
            "shqk,skhd->sqhd", d_scores, key_block, preferred_element_type=jnp.float32
        )
        d_key_part = (
            jnp.einsum("shqk,sqhd->skhd", d_scores, query_h, preferred_element_type=jnp.float32)
            * score_scale
        )
        d_value_part = jnp.einsum(
            "shqk,sqhd->skhd", soft_b, grad_h, preferred_element_type=jnp.float32
        )
        return (carried, (d_key_part, d_value_part))

    d_query_h, (key_parts, value_parts) = lax.scan(query_and_key, head_zeros, block_ids)
    key_terms = jnp.moveaxis(key_parts, 0, 1).reshape(num_seqs, length, H * HS)
    value_terms = jnp.moveaxis(value_parts, 0, 1).reshape(num_seqs, length, H * HS)
    d_key_own, d_value_own = (
        lax.psum_scatter(
            key_terms.astype(jnp.bfloat16), "seq", scatter_dimension=1, tiled=True
        ).astype(jnp.float32),
        lax.psum_scatter(
            value_terms.astype(jnp.bfloat16), "seq", scatter_dimension=1, tiled=True
        ).astype(jnp.float32),
    )
    d_query_rot = d_query_h.reshape(num_seqs, own_tokens, H * HS) * score_scale
    d_query = rotate(d_query_rot, cosine, -sine_t).astype(jnp.bfloat16)
    d_key = rotate(d_key_own, cosine, -sine_t).astype(jnp.bfloat16)
    d_value = (0.5 * d_value_own).astype(jnp.bfloat16)
    grad_query = weight_grad(normed_one, d_query)
    grad_key = weight_grad(normed_one, d_key)
    grad_value = weight_grad(normed_one, d_value)
    d_normed_one = (
        project_back(d_query, reused[0])
        + project_back(d_key, reused[1])
        + project_back(d_value, reused[2])
    )
    norm_pull_one = jax.vjp(normalize, input_f, gain_one)[1]
    d_input_part, d_gain_one = norm_pull_one(d_normed_one)
    d_input = (d_hidden + d_input_part).astype(jnp.bfloat16)
    owned = (
        lax.psum_scatter(
            grad_query.astype(jnp.bfloat16), "seq", scatter_dimension=0, tiled=True
        ).astype(jnp.float32),
        lax.psum_scatter(
            grad_key.astype(jnp.bfloat16), "seq", scatter_dimension=0, tiled=True
        ).astype(jnp.float32),
        lax.psum_scatter(
            grad_value.astype(jnp.bfloat16), "seq", scatter_dimension=0, tiled=True
        ).astype(jnp.float32),
        lax.psum_scatter(
            grad_out.astype(jnp.bfloat16), "seq", scatter_dimension=0, tiled=True
        ).astype(jnp.float32),
        lax.psum_scatter(
            grad_gate.astype(jnp.bfloat16), "seq", scatter_dimension=0, tiled=True
        ).astype(jnp.float32),
        lax.psum_scatter(
            grad_up.astype(jnp.bfloat16), "seq", scatter_dimension=0, tiled=True
        ).astype(jnp.float32),
        lax.psum_scatter(
            grad_down.astype(jnp.bfloat16), "seq", scatter_dimension=0, tiled=True
        ).astype(jnp.float32),
    )
    final_set = (
        lax.psum_scatter(
            owned[0].astype(jnp.bfloat16), "dp", scatter_dimension=1, tiled=True
        ).astype(jnp.float32),
        lax.psum_scatter(
            owned[1].astype(jnp.bfloat16), "dp", scatter_dimension=1, tiled=True
        ).astype(jnp.float32),
        lax.psum_scatter(
            owned[2].astype(jnp.bfloat16), "dp", scatter_dimension=1, tiled=True
        ).astype(jnp.float32),
        lax.psum_scatter(
            owned[3].astype(jnp.bfloat16), "dp", scatter_dimension=1, tiled=True
        ).astype(jnp.float32),
        lax.psum_scatter(
            owned[4].astype(jnp.bfloat16), "dp", scatter_dimension=1, tiled=True
        ).astype(jnp.float32),
        lax.psum_scatter(
            owned[5].astype(jnp.bfloat16), "dp", scatter_dimension=1, tiled=True
        ).astype(jnp.float32),
        lax.psum_scatter(
            owned[6].astype(jnp.bfloat16), "dp", scatter_dimension=1, tiled=True
        ).astype(jnp.float32),
    )
    square_sums, gain_sums = lax.psum((squares, jnp.stack([d_gain_one, d_gain_two])), ("dp", "seq"))
    cell_count = num_seqs * own_tokens * model_width * lax.axis_size("dp") * lax.axis_size("seq")
    root_mean = jnp.sqrt(square_sums / cell_count)
    share = model_width // lax.axis_size("seq")
    gain_grads = lax.dynamic_slice_in_dim(gain_sums, lax.axis_index("seq") * share, share, 1)
    return (
        result.astype(jnp.bfloat16),
        d_input,
        d_value,
        gain_grads[0],
        final_set[0],
        final_set[1],
        final_set[2],
        final_set[3],
        gain_grads[1],
        final_set[4],
        final_set[5],
        final_set[6],
        root_mean,
    )


def general_solution(mesh):
    in_specs = (
        P("dp", "seq", None),
        P("dp", "seq", None),
        P("dp", "seq", None),
        P("dp", None),
        P("seq"),
        P("seq", "dp"),
        P("seq", "dp"),
        P("seq", "dp"),
        P("seq", "dp"),
        P("seq"),
        P("seq", "dp"),
        P("seq", "dp"),
        P("seq", "dp"),
    )
    out_specs = (
        P("dp", "seq", None),
        P("dp", "seq", None),
        P("dp", "seq", None),
        P("seq"),
        P("seq", "dp"),
        P("seq", "dp"),
        P("seq", "dp"),
        P("seq", "dp"),
        P("seq"),
        P("seq", "dp"),
        P("seq", "dp"),
        P("seq", "dp"),
        P(),
    )
    return jax.shard_map(local, mesh=mesh, in_specs=in_specs, out_specs=out_specs, check_vma=False)


T = 4
Z = 4
BF = jnp.bfloat16
F32 = jnp.float32


def flip_c(v):
    return lax.ppermute(v, "c", [(0, 1), (1, 0)])


def flip_x(v):
    return lax.ppermute(v, "x", [(0, 1), (1, 0)])


def flip_y(v):
    return lax.ppermute(v, "y", [(0, 1), (1, 0)])


def flip_xc(v):
    return lax.ppermute(v, ("x", "c"), [(i, i ^ 3) for i in range(4)])


def shift_z(v, k):
    if k % Z == 0:
        return v
    return lax.ppermute(v, "z", [(i, (i + k) % Z) for i in range(Z)])


def pick(stacked, index):
    return lax.dynamic_index_in_dim(stacked, index, 0, keepdims=False)


def put(buffer, piece, *index):
    rest = buffer.ndim - len(index)
    piece = piece.reshape((1,) * len(index) + buffer.shape[len(index):])
    return lax.dynamic_update_slice(buffer, piece, tuple(index) + (0,) * rest)


def spread(rows):
    across = flip_x(rows)
    return [rows, flip_c(rows), across, flip_c(across)]


def collect(parts):
    sent = jnp.stack([parts[1].astype(BF), parts[3].astype(BF)])
    got = flip_c(sent).astype(F32)
    far = parts[2] + got[1]
    return parts[0] + got[0] + flip_x(far.astype(BF)).astype(F32)


def swap_four(stacked, j):
    moves = (lambda v: v, flip_c, flip_x, flip_xc)
    return [moves[r](pick(stacked, j ^ r)) for r in range(T)]


def natural_four(parts, j):
    buffer = jnp.zeros((T,) + parts[0].shape, parts[0].dtype)
    for r in range(T):
        buffer = put(buffer, parts[r], j ^ r)
    return buffer


def dot_tn(left, right):
    return lax.dot_general(left, right, (((0,), (0,)), ((), ())), preferred_element_type=F32)


def dot_nt(left, right):
    return lax.dot_general(left, right, (((1,), (1,)), ((), ())), preferred_element_type=F32)


def dot_tt(left, right):
    return lax.dot_general(left, right, (((0,), (1,)), ((), ())), preferred_element_type=F32)


def dot_nn(left, right):
    return lax.dot_general(left, right, (((1,), (0,)), ((), ())), preferred_element_type=F32)


BQ = 512
BK = 512
LB = 128


def mask_block(start, q0, k0):
    key = k0 + lax.broadcasted_iota(jnp.int32, (BK, BQ), 0)
    query = q0 + lax.broadcasted_iota(jnp.int32, (BK, BQ), 1)
    return (key >= start) & (key <= query)


def attend_kernel(info, start_ref, qkv_ref, o_ref, of_ref, lse_ref, q_t, k_n, v_t):
    length = q_t.shape[1]
    blocks = length // LB
    per = qkv_ref.shape[2] // LB
    j = info[0]

    @pl.loop(0, blocks)
    def _(n):
        z = n // per
        lanes = pl.ds(pl.multiple_of(((n % per) ^ j) * LB, LB), LB)
        to = pl.ds(pl.multiple_of(n * LB, LB), LB)
        q_t[:, to] = qkv_ref[z, 0:HS, lanes]
        k_n[to, :] = qkv_ref[z, HS:2 * HS, lanes].T
        v_t[:, to] = qkv_ref[z, 2 * HS:3 * HS, lanes]

    for i in range(length // BQ):
        q0 = i * BQ
        qb = q_t[:, q0:q0 + BQ]
        start = start_ref[:, q0:q0 + BQ]

        def step(kb, carried):
            top, total, acc = carried
            k0 = pl.multiple_of(kb * BK, BK)
            s = dot_nn(k_n[pl.ds(k0, BK), :], qb)
            s = jnp.where(mask_block(start, q0, k0), s, -1e30)
            new_top = jnp.maximum(top, jnp.max(s, axis=0, keepdims=True))
            p = jnp.exp(s - new_top)
            alpha = jnp.exp(top - new_top)
            total = total * alpha + jnp.sum(p, axis=0, keepdims=True)
            acc = acc * alpha + dot_nn(v_t[:, pl.ds(k0, BK)], p.astype(BF))
            return new_top, total, acc

        init = (
            jnp.full((1, BQ), -1e30, F32),
            jnp.zeros((1, BQ), F32),
            jnp.zeros((HS, BQ), F32),
        )
        top, total, acc = lax.fori_loop(info[1 + i] // BK, (q0 + BQ - 1) // BK + 1, step, init)
        of_ref[:, q0:q0 + BQ] = acc / total
        lse_ref[:, q0:q0 + BQ] = top + jnp.log(total)

    @pl.loop(0, blocks)
    def _(n):
        z = n // per
        lanes = pl.ds(pl.multiple_of(((n % per) ^ j) * LB, LB), LB)
        to = pl.ds(pl.multiple_of(n * LB, LB), LB)
        o_ref[z, :, lanes] = of_ref[:, to].astype(BF)


def unrotate(value, cosine, sine_t):
    half_size = HS // 2
    low = value[:half_size]
    high = value[half_size:]
    return jnp.concatenate([low * cosine + high * sine_t, high * cosine - low * sine_t], axis=0)


def attend_back_kernel(
    info, start_ref, cos_ref, sin_ref, qkv_ref, do_ref, of_ref, lse_ref, d_ref,
    q_t, q_n, k_t, k_n, v_n, do_t, do_n, dq_t, dk_n, dv_n,
):
    length = q_t.shape[1]
    blocks = length // LB
    per = qkv_ref.shape[2] // LB
    j = info[0]

    @pl.loop(0, blocks)
    def _(n):
        z = n // per
        lanes = pl.ds(pl.multiple_of(((n % per) ^ j) * LB, LB), LB)
        to = pl.ds(pl.multiple_of(n * LB, LB), LB)
        q_b = qkv_ref[z, 0:HS, lanes]
        k_b = qkv_ref[z, HS:2 * HS, lanes]
        do_b = do_ref[z, :, lanes]
        q_t[:, to] = q_b
        q_n[to, :] = q_b.T
        k_t[:, to] = k_b
        k_n[to, :] = k_b.T
        v_n[to, :] = qkv_ref[z, 2 * HS:3 * HS, lanes].T
        do_t[:, to] = do_b
        do_n[to, :] = do_b.T
        dk_n[to, :] = jnp.zeros((LB, HS), F32)
        dv_n[to, :] = jnp.zeros((LB, HS), F32)

    for i in range(length // BQ):
        q0 = i * BQ
        qb = q_t[:, q0:q0 + BQ]
        q_rows = q_n[q0:q0 + BQ, :]
        dob = do_t[:, q0:q0 + BQ]
        do_rows = do_n[q0:q0 + BQ, :]
        start = start_ref[:, q0:q0 + BQ]
        lse = lse_ref[:, q0:q0 + BQ]
        delta = jnp.sum(of_ref[:, q0:q0 + BQ] * dob.astype(F32), axis=0, keepdims=True)

        def step(kb, acc):
            k0 = pl.multiple_of(kb * BK, BK)
            rows = pl.ds(k0, BK)
            s = dot_nn(k_n[rows, :], qb)
            s = jnp.where(mask_block(start, q0, k0), s, -1e30)
            p = jnp.exp(s - lse)
            dp = dot_nn(v_n[rows, :], dob)
            ds = (p * (dp - delta)).astype(BF)
            dv_n[rows, :] += dot_nn(p.astype(BF), do_rows)
            dk_n[rows, :] += dot_nn(ds, q_rows)
            return acc + dot_nn(k_t[:, rows], ds)

        dq_t[:, q0:q0 + BQ] = lax.fori_loop(
            info[1 + i] // BK, (q0 + BQ - 1) // BK + 1, step, jnp.zeros((HS, BQ), F32)
        )

    @pl.loop(0, blocks)
    def _(n):
        z = n // per
        lanes = pl.ds(pl.multiple_of(((n % per) ^ j) * LB, LB), LB)
        to = pl.ds(pl.multiple_of(n * LB, LB), LB)
        cosine = cos_ref[:, to]
        sine_t = sin_ref[:, to]
        d_ref[z, 0:HS, lanes] = unrotate(dq_t[:, to] * (HS ** -0.5), cosine, sine_t).astype(BF)
        d_ref[z, HS:2 * HS, lanes] = unrotate(dk_n[to, :].T, cosine, sine_t).astype(BF)
        d_ref[z, 2 * HS:3 * HS, lanes] = (0.5 * dv_n[to, :].T).astype(BF)


def vmem_call(body, out_shape, scratch, flops, exps, name):
    def run(info, *arrays):
        spec = pl.BlockSpec(memory_space=pltpu.VMEM)
        moved = sum(a.size * a.dtype.itemsize for a in arrays)
        return pl.pallas_call(
            body,
            out_shape=out_shape,
            in_specs=[pl.BlockSpec(memory_space=pltpu.SMEM)] + [spec] * len(arrays),
            out_specs=jax.tree.map(lambda _: spec, out_shape),
            scratch_shapes=scratch,
            cost_estimate=pl.CostEstimate(
                flops=flops, bytes_accessed=2 * moved, transcendentals=exps
            ),
            name=name,
        )(info, *arrays)

    return run


def attend(info, start, qkv):
    length = start.shape[1]
    out_shape = (
        jax.ShapeDtypeStruct((Z, HS, length // Z), BF),
        jax.ShapeDtypeStruct((HS, length), F32),
        jax.ShapeDtypeStruct((1, length), F32),
    )
    scratch = [
        pltpu.VMEM((HS, length), BF),
        pltpu.VMEM((length, HS), BF),
        pltpu.VMEM((HS, length), BF),
    ]
    pairs = length * length // 2
    return vmem_call(attend_kernel, out_shape, scratch, 4 * HS * pairs, pairs, "attend")(
        info, start, qkv
    )


def attend_back(info, start, cosine, sine_t, qkv, d_out, out_f, lse):
    length = start.shape[1]
    out_shape = jax.ShapeDtypeStruct((Z, 3 * HS, length // Z), BF)
    wide, tall = (HS, length), (length, HS)
    scratch = [
        pltpu.VMEM(wide, BF), pltpu.VMEM(tall, BF), pltpu.VMEM(wide, BF), pltpu.VMEM(tall, BF),
        pltpu.VMEM(tall, BF), pltpu.VMEM(wide, BF), pltpu.VMEM(tall, BF),
        pltpu.VMEM(wide, F32), pltpu.VMEM(tall, F32), pltpu.VMEM(tall, F32),
    ]
    pairs = length * length // 2
    return vmem_call(
        attend_back_kernel, out_shape, scratch, 10 * HS * pairs, pairs, "attend_back"
    )(info, start, cosine, sine_t, qkv, d_out, out_f, lse)


def inverse_rms(rows_in):
    return lax.rsqrt(jnp.mean(rows_in * rows_in, axis=-1, keepdims=True) + EPSILON)


def norm_back(rows_in, gain, grad):
    r = inverse_rms(rows_in)
    u = rows_in * r
    scaled = gain * grad
    d_rows = r * (scaled - u * jnp.mean(u * scaled, axis=-1, keepdims=True))
    return d_rows, jnp.sum(grad * u, axis=0)


def gather_rows(pieces, y, z):
    rows, columns = pieces[0].shape
    buffer = jnp.zeros((2, Z, rows, columns), BF)
    for k in range(Z):
        plane = (z - k) % Z
        buffer = put(buffer, pieces[k], y, plane)
        buffer = put(buffer, flip_y(pieces[k]), 1 - y, plane)
    return buffer.reshape(2, Z * rows, columns)


def scatter_rows(partial, y, z):
    _, height, columns = partial.shape
    mine = pick(partial, y) + flip_y(pick(partial, 1 - y).astype(BF)).astype(F32)
    blocks = mine.reshape(Z, height // Z, columns)
    total = pick(blocks, z)
    for k in range(1, Z):
        total = total + shift_z(pick(blocks, (z + k) % Z).astype(BF), k).astype(F32)
    return total


def fast_local(
    layer_input, v_first, cotangent, segments, norm1_gain, w_query, w_key, w_value, w_out,
    norm2_gain, w_gate, w_up, w_down,
):
    _, own, width = layer_input.shape
    length = segments.shape[1]
    plane_tokens = length // Z
    y, z = lax.axis_index("y"), lax.axis_index("z")
    j = 2 * lax.axis_index("x") + lax.axis_index("c")
    rows64 = w_query.shape[0]
    units = w_gate.shape[1] // (2 * T)
    barrier = lax.optimization_barrier

    x_own, cot_own = layer_input[0], cotangent[0]

    def by_rank(weight, size):
        return weight.reshape(weight.shape[0], 2, T, size).transpose(2, 0, 1, 3)

    qkv_w = jnp.stack([by_rank(w, HS) for w in (w_query, w_key, w_value)], axis=3)
    qkv_w = qkv_w.reshape(T, rows64, 6 * HS)
    qkv_piece = natural_four(swap_four(qkv_w, j), j).reshape(T * rows64, 6 * HS)
    qkv_pieces = [shift_z(qkv_piece, k) for k in range(Z)]
    w_qkv = gather_rows(qkv_pieces, y, z)

    gains = jnp.concatenate([norm1_gain, norm2_gain]).reshape(1, 2 * rows64)
    gain_rel = [natural_four(spread(gains), j)]
    gain_rel = [shift_z(gain_rel[0], k) for k in range(Z)]
    gain_all = jnp.zeros((Z,) + gain_rel[0].shape, BF)
    for k in range(Z):
        gain_all = put(gain_all, gain_rel[k], (z - k) % Z)
    gain_all = gain_all.reshape(Z * T, 2, rows64).transpose(1, 0, 2).reshape(2, width).astype(F32)
    gain_one, gain_two = gain_all[0], gain_all[1]

    x_four = jnp.concatenate(spread(x_own))
    v_t = v_first[0].reshape(own, Z, T, HS).transpose(2, 1, 3, 0).reshape(T, Z * HS, own)
    v_four = jnp.concatenate(swap_four(v_t, j), axis=1)

    seg = segments[0]
    start = jnp.zeros_like(seg)
    for d in range(3):
        start = start + jnp.where(seg > d, jnp.sum((seg == d).astype(jnp.int32)), 0)
    index = jnp.arange(length, dtype=jnp.int32)
    half_size = HS // 2
    frequency = 10000.0 ** (-jnp.arange(half_size, dtype=F32) * 2.0 / HS)
    angles = frequency[:, None] * (index - start).astype(F32)[None, :]
    cosine, sine_t = jnp.cos(angles), jnp.sin(angles)
    start_row = start[None, :]
    info = jnp.concatenate([j[None].astype(jnp.int32), start[::BQ]])
    plane_cos = lax.dynamic_slice_in_dim(cosine, z * plane_tokens, plane_tokens, 1)
    plane_sin = lax.dynamic_slice_in_dim(sine_t, z * plane_tokens, plane_tokens, 1)

    def arrived(table):
        parts = [
            lax.dynamic_slice_in_dim(table, (j ^ r) * own, own, 1) for r in range(T)
        ]
        return jnp.concatenate(parts, axis=1)

    cos_four, sin_four = arrived(plane_cos), arrived(plane_sin)

    x_f = x_four.astype(F32)
    normed_one = (x_f * inverse_rms(x_f) * gain_one).astype(BF)

    def turned(half):
        raw = dot_tt(w_qkv[half], normed_one).reshape(2, 3, HS, T * own)
        low, high = raw[:, :2, :half_size], raw[:, :2, half_size:]
        rot = jnp.concatenate(
            [low * cos_four - high * sin_four, high * cos_four + low * sin_four], axis=2
        )
        values = v_four.reshape(2, 2, HS, T * own)[half].astype(F32)
        mixed = 0.5 * raw[:, 2] + 0.5 * values
        return jnp.stack([rot[:, 0] * (HS ** -0.5), rot[:, 1], mixed], axis=1).astype(BF)

    heads = jnp.concatenate([turned(0), turned(1)]).reshape(Z, 3 * HS, T * own)

    def to_heads(stacked):
        buffer = jnp.zeros_like(stacked)
        for k in range(Z):
            buffer = put(buffer, shift_z(pick(stacked, (z + k) % Z), k), (z - k) % Z)
        return buffer

    qkv = to_heads(heads)
    attended_z, attended_f, lse = attend(info, start_row, qkv)
    attended = to_heads(attended_z).reshape(Z * HS, T * own)

    out_src, gate_src, up_src, down_src, _ = barrier(
        (w_out, w_gate, w_up, w_down, tuple(qkv_pieces))
    )
    w_out_all = gather_rows([shift_z(out_src, k) for k in range(Z)], y, z)
    pair_w = jnp.stack([by_rank(gate_src, units), by_rank(up_src, units)], axis=1)
    pair_w = pair_w.reshape(T, 2 * rows64, 2 * units)
    pair_four = natural_four(swap_four(pair_w, j), j).reshape(T, 2, rows64, 2 * units)
    pair_four = pair_four.transpose(1, 0, 2, 3).reshape(2, T * rows64, 2 * units)
    w_gate_all = gather_rows([shift_z(pair_four[0], k) for k in range(Z)], y, z)
    w_up_all = gather_rows([shift_z(pair_four[1], k) for k in range(Z)], y, z)
    w_down_all = gather_rows([shift_z(down_src, k) for k in range(Z)], y, z)

    def both(make):
        return jnp.concatenate([make(0), make(1)], axis=1)

    branch_part = both(lambda h: dot_tn(attended, w_out_all[h]))

    def split(rows):
        return [rows[r * own:(r + 1) * own] for r in range(T)]

    branch_a = collect(split(branch_part))
    x_own_f = x_own.astype(F32)
    hidden_in = x_own_f + branch_a
    normed_two = (hidden_in * inverse_rms(hidden_in) * gain_two).astype(BF)
    normed_four = jnp.concatenate(spread(normed_two))
    cot_four = jnp.concatenate(spread(cot_own))

    half_width = width // 2
    cot_halves = (cot_four[:, :half_width], cot_four[:, half_width:])

    step = 2 * units
    branch_m_parts = []
    d_normed_part = 0.0
    grads_gate, grads_up, grads_down = [], [], []
    for h in range(2):
        down_h = [w_down_all[e, h * step:(h + 1) * step] for e in range(2)]
        gate = dot_nn(normed_four, w_gate_all[h])
        up = dot_nn(normed_four, w_up_all[h])
        sigma = jax.nn.sigmoid(gate)
        silu = gate * sigma
        active = (silu * up).astype(BF)
        branch_m_parts.append(both(lambda e: dot_nn(active, down_h[e])))
        d_active = dot_nt(cot_halves[0], down_h[0]) + dot_nt(cot_halves[1], down_h[1])
        d_gate = (d_active * up * sigma * (1.0 + gate * (1.0 - sigma))).astype(BF)
        d_up = (d_active * silu).astype(BF)
        d_normed_part = (
            d_normed_part + dot_nt(d_gate, w_gate_all[h]) + dot_nt(d_up, w_up_all[h])
        )
        grads_gate.append(dot_tn(normed_four, d_gate))
        grads_up.append(dot_tn(normed_four, d_up))
        grads_down.append(jnp.stack([dot_tn(active, c) for c in cot_halves]))

    d_normed_two = collect(split(d_normed_part))
    d_hidden_part, d_gain_two = norm_back(hidden_in, gain_two, d_normed_two)
    d_hidden = cot_own.astype(F32) + d_hidden_part
    d_branch_four = jnp.concatenate(spread(d_hidden.astype(BF)))
    d_branch_halves = (d_branch_four[:, :half_width], d_branch_four[:, half_width:])
    d_attended = (
        dot_nt(w_out_all[0], d_branch_halves[0]) + dot_nt(w_out_all[1], d_branch_halves[1])
    ).astype(BF)
    d_out = to_heads(d_attended.reshape(Z, HS, T * own))
    d_heads = attend_back(info, start_row, cosine, sine_t, qkv, d_out, attended_f, lse)
    d_qkv = to_heads(d_heads)
    d_qkv_halves = d_qkv.reshape(2, 6 * HS, T * own)

    grads_qkv = jnp.stack([dot_tt(normed_one, d_qkv_halves[h]) for h in range(2)])
    d_one_part = dot_tt(d_qkv_halves[0], w_qkv[0]) + dot_tt(d_qkv_halves[1], w_qkv[1])
    d_normed_one = collect(split(d_one_part))
    d_input_part, d_gain_one = norm_back(x_own_f, gain_one, d_normed_one)
    d_input = (d_hidden + d_input_part).astype(BF)

    branch_m = collect(split(branch_m_parts[0] + branch_m_parts[1]))
    result = hidden_in + branch_m
    squares = jnp.stack(
        [jnp.sum(result * result), jnp.sum(branch_a * branch_a), jnp.sum(branch_m * branch_m)]
    )

    d_values = d_qkv[:, 2 * HS:].reshape(Z * HS, T, own).transpose(1, 0, 2)
    moves = (lambda v: v, flip_c, flip_x, flip_xc)
    d_values = natural_four([moves[r](d_values[r]) for r in range(T)], j)
    d_v_first = d_values.reshape(T, Z, HS, own).transpose(3, 1, 0, 2).reshape(1, own, width)

    def home(total, height, size):
        stacked = total.reshape(T, height, total.shape[1]).astype(BF)
        return natural_four(swap_four(stacked, j), j).astype(F32)

    def columns(four, size):
        return four.reshape(T, four.shape[1], 2, size).transpose(1, 2, 0, 3).reshape(
            four.shape[1], 2 * T * size
        )

    gate_total = scatter_rows(jnp.stack(grads_gate), y, z)
    up_total = scatter_rows(jnp.stack(grads_up), y, z)
    down_total = scatter_rows(
        jnp.concatenate([grads_down[0], grads_down[1]], axis=1), y, z
    )
    out_total = scatter_rows(
        jnp.stack([dot_nn(attended, d) for d in d_branch_halves]), y, z
    )
    qkv_total = scatter_rows(grads_qkv, y, z)
    d_w_gate = columns(home(gate_total, rows64, units), units)
    d_w_up = columns(home(up_total, rows64, units), units)
    qkv_home = home(qkv_total, rows64, HS).reshape(T, rows64, 2, 3, HS)
    d_w_qkv = [columns(qkv_home[:, :, :, m].reshape(T, rows64, 2 * HS), HS) for m in range(3)]

    packed = jnp.concatenate(
        [d_gain_one, d_gain_two, squares, jnp.zeros((LB - 3,), F32)]
    ).reshape(-1, LB)
    for move in (flip_c, flip_x, flip_y):
        packed = packed + move(packed)
    for bit in (1, 2):
        packed = packed + lax.ppermute(packed, "z", [(i, i ^ bit) for i in range(Z)])
    flat = packed.reshape(-1)
    cells = length * width * 2
    root_mean = jnp.sqrt(flat[2 * width:2 * width + 3] / cells)
    first = (z * T + j) * rows64
    gain_one_grad = lax.dynamic_slice_in_dim(flat, first, rows64, 0)
    gain_two_grad = lax.dynamic_slice_in_dim(flat, width + first, rows64, 0)

    return (
        result.astype(BF)[None],
        d_input[None],
        d_v_first,
        gain_one_grad,
        d_w_qkv[0],
        d_w_qkv[1],
        d_w_qkv[2],
        out_total,
        gain_two_grad,
        d_w_gate,
        d_w_up,
        down_total,
        root_mean,
    )


def fast_solution(mesh):
    grid = Mesh(mesh.devices.reshape(2, Z, 2, 2), ("y", "z", "x", "c"))
    rows = ("z", "x", "c")
    tokens, square, flat = P("y", rows, None), P(rows, "y"), P(rows)
    in_specs = (
        tokens, tokens, tokens, P("y", None), flat, square, square, square, square, flat,
        square, square, square,
    )
    out_specs = (
        tokens, tokens, tokens, flat, square, square, square, square, flat, square, square,
        square, P(),
    )
    return jax.shard_map(
        fast_local, mesh=grid, in_specs=in_specs, out_specs=out_specs, check_vma=False
    )


def solution(mesh):
    if mesh.shape["dp"] == 2 and mesh.shape["seq"] == Z * T == H:
        return fast_solution(mesh)
    return general_solution(mesh)
```
